32 devices in a mesh: src: 8 (over z, y), snk: 4 (over x, core).
Axes of the slice: x: 2, y: 2, z: 4, core: 2. Of those that a mesh axis runs over, the one named last changes fastest.
Arguments:
- tau_cols: bfloat16 [2, 8, 8, 256, 256], P(None, 'src', None, 'snk'), may hold values from -0.25 to 0.25
- elementals: bfloat16 [256, 2, 256, 256], P('src'), may hold values from -0.25 to 0.25
- need_ids: int32 [8, 8], replicated, may hold values from 0 to 255, as said below
- diagrams: int32 [8, 8, 3], P('src'), may hold values from 0 to 15, as said below
- phases: int32 [16], replicated, may hold values from 0 to 3
- block_sizes: int32 [4], replicated, may hold values from 1 to 3, 8 in all
Outputs:
- correlators: float32 [8, 4, 3, 2, 8], P('src', 'snk')
The draws below stay inside these ranges and needn't reach their ends.
Inputs may be any that keep to these rules, and one draw needn't show every extreme that they name: `block_sizes`: the sizes sum to 8, and one of them is exactly 3. `need_ids`: the 8 ids of a row are distinct. `diagrams`: entry 0 of a diagram is below 4, entry 1 below 4, entry 2 below 16; each of a row's 4 sink-side and 4 source-side entries is named by some diagram of the row.
All inputs are finite; a program needn't handle non-finite values.
Results may differ from the reference program's by a relative error of at most 0.004.
Values may be sent and summed in bfloat16 or wider, within the bound.
A program may use at most 64 MiB of HBM per device.

```python
import math
import jax
import jax.numpy as jnp
import numpy as np
from jax import lax

NV = 256
NE = 256
NSN = 4
NSR = 4
NI = 8
NDIAG = 8
NGAM = 16
MAXB = 3
TSNK = 8
TSRC = 8
N_SRC = 8
N_SNK = 4


def draw_need_ids(key, part):
    row_keys = jax.random.split(key, N_SRC)

    def one_row(row_key):
        return jax.random.permutation(row_key, NE)[:NI].astype(jnp.int32)
    table_rows = jax.vmap(one_row)(row_keys)
    leading = jnp.array([NE - 1, 0], dtype=jnp.int32)
    middle = (jax.random.permutation(jax.random.fold_in(key, 7), NE - 2)[:NI - 2] + 1).astype(jnp.int32)
    return table_rows.at[0].set(jnp.concatenate([leading, middle]))


def draw_diagrams(key, part):
    first_key, second_key, third_key, fourth_key = jax.random.split(jax.random.fold_in(key, 11), 4)
    places = jnp.arange(NDIAG, dtype=jnp.int32)[None, :]
    sink_free = jax.random.randint(first_key, (N_SRC, NDIAG), 0, NSN, dtype=jnp.int32)
    source_free = jax.random.randint(second_key, (N_SRC, NDIAG), 0, NSR, dtype=jnp.int32)
    rotation = jax.random.randint(third_key, (N_SRC, 1), 0, NSR, dtype=jnp.int32)
    sink_column = jnp.where(places < NSN, places % NSN, sink_free)
    source_column = jnp.where(places < NSR, (places + rotation) % NSR, source_free)
    gamma_column = jax.random.randint(fourth_key, (N_SRC, NDIAG), 0, NGAM, dtype=jnp.int32)
    gamma_column = gamma_column.at[0, 0].set(NGAM - 1)
    return jnp.stack([sink_column, source_column, gamma_column], axis=2).astype(jnp.int32)


def place_ends(values, stream_key, low, high):
    longest = values.shape.index(max(values.shape))
    spots = []
    for shift in (0, 1):
        where = [jax.random.randint(jax.random.fold_in(stream_key, axis), (), 0, length) for axis, length in enumerate(values.shape)]
        where[longest] = (where[longest] + shift) % values.shape[longest]
        spots.append(tuple(where))
    return values.at[spots[0]].set(low).at[spots[1]].set(high)


def level_of(own_key, extent, pieces, low, top_value):
    def one(axis_at, shards_of):
        heights = jax.random.uniform(jax.random.fold_in(jax.random.fold_in(own_key, 6), axis_at), (shards_of,), jnp.float32, low / len(pieces), top_value / len(pieces))
        return jnp.repeat(jnp.exp(heights), extent[axis_at] // shards_of).reshape((-1,) + (1,) * (len(extent) - axis_at - 1))

    level = one(*pieces[0])
    for cut in pieces[1:]:
        level = level * one(*cut)
    return level


def split_up(number_of, total, most, skew):
    weights = [(1 << 20) // math.isqrt(rank ** skew) + 1 for rank in range(2, number_of + 1)]
    spare, holding = total - most - (number_of - 1), [1] * (number_of - 1)
    while spare > 0:
        movable = [i for i in range(number_of - 1) if holding[i] < most]
        mass, left = sum([weights[i] for i in movable]), spare
        for i in movable:
            addition = min(most - holding[i], max(1, left * weights[i] // mass), spare)
            holding[i] = holding[i] + addition
            spare = spare - addition
    return np.array([most] + holding)


def ragged_sizes(key, amount, total, bound, lean):
    if amount == 2:
        one = jax.random.randint(key, (), max(1, total - bound), min(bound, total - 1) + 1)
        return jnp.stack([one, total - one])
    sizes = jnp.asarray(split_up(amount, total, bound, lean), jnp.int32)
    twos = (amount - 1) // 2
    source_of, taker = sizes[1:1 + 2 * twos:2], sizes[2:2 + 2 * twos:2]
    margin = jnp.minimum(source_of - 1, bound - taker)
    shifted = jax.random.randint(jax.random.fold_in(key, 1), (twos,), 0, 1 << 20) % (margin + 1)
    sizes = sizes.at[1:1 + 2 * twos:2].set(source_of - shifted).at[2:2 + 2 * twos:2].set(taker + shifted)
    return sizes[jax.random.permutation(jax.random.fold_in(key, 2), amount)]


def bell_draw(own_key, extent, deviation, most, shards=(), kind=jnp.bfloat16):
    loudness = level_of(own_key, extent, shards, -0.22, 0.18) if shards else 1.0
    drawn = jax.random.normal(own_key, extent, jnp.float32) * deviation * loudness
    return jnp.minimum(jnp.maximum(drawn, -most), most).astype(kind)


def setup_inputs(seed: int = 0) -> dict:
    splits = jax.random.split(jax.random.key(seed), 7)
    return {
        "tau_cols": bell_draw(splits[0], (2, TSRC, TSNK, NV, NV), (2 * NV) ** -0.5, 0.25, ((1, 8), (3, 4))),
        "elementals": bell_draw(splits[1], (NV, 2, NE, NV), (2 * NV) ** -0.5, 0.25, ((0, 8),)),
        "need_ids": draw_need_ids(jax.random.fold_in(splits[6], 71), 0),
        "diagrams": draw_diagrams(jax.random.fold_in(splits[6], 71), 0),
        "phases": place_ends(jax.random.randint(splits[4], (NGAM,), 0, 4), jax.random.fold_in(splits[4], 1), 0, 3).astype(jnp.int32),
        "block_sizes": ragged_sizes(splits[5], N_SNK, TSNK, MAXB, 2).astype(jnp.int32),
    }


def slot_values(elemental_items, tau_slot, diagram_rows, phases):
    real_part = tau_slot[0]
    imag_part = tau_slot[1]
    left_stack = jnp.stack([jnp.stack([real_part, imag_part]), jnp.stack([-imag_part, real_part])]).astype(jnp.float32)
    right_stack = jnp.stack([jnp.stack([real_part, -imag_part]), jnp.stack([imag_part, real_part])]).astype(jnp.float32)
    items_wide = elemental_items.astype(jnp.float32)
    left_node = lax.dot_general(items_wide[:, :, :NSN], left_stack, (((1, 3), (0, 3)), ((), ())), precision=lax.Precision.HIGHEST)
    left_node = lax.optimization_barrier(left_node.astype(jnp.bfloat16)).astype(jnp.float32)
    right_node = lax.dot_general(items_wide[:, :, NSN:], right_stack, (((1, 3), (0, 2)), ((), ())), precision=lax.Precision.HIGHEST)
    right_node = lax.optimization_barrier(right_node.astype(jnp.bfloat16)).astype(jnp.float32)
    pair_sums = lax.dot_general(left_node, right_node, (((0, 3), (3, 0)), ((), ())), precision=lax.Precision.HIGHEST)
    pair_real = pair_sums[:, 0, :, 0] - pair_sums[:, 1, :, 1]
    pair_imag = pair_sums[:, 0, :, 1] + pair_sums[:, 1, :, 0]
    chosen_real = pair_real[diagram_rows[:, 0], diagram_rows[:, 1]]
    chosen_imag = pair_imag[diagram_rows[:, 0], diagram_rows[:, 1]]
    quarter = phases[diagram_rows[:, 2]]
    cosine = (quarter == 0).astype(jnp.float32) - (quarter == 2).astype(jnp.float32)
    sine_part = (quarter == 1).astype(jnp.float32) - (quarter == 3).astype(jnp.float32)
    return jnp.stack([cosine * chosen_real - sine_part * chosen_imag, sine_part * chosen_real + cosine * chosen_imag])


def reference(tau_cols, elementals, need_ids, diagrams, phases, block_sizes):
    def per_source(source):
        elemental_items = jnp.take(elementals, need_ids[source], axis=2)
        diagram_rows = diagrams[source]
        source_tau = lax.dynamic_index_in_dim(tau_cols, source, axis=1, keepdims=False)

        def per_time(sink_time):
            tau_slot = lax.dynamic_index_in_dim(source_tau, sink_time, axis=1, keepdims=False)
            return slot_values(elemental_items, tau_slot, diagram_rows, phases)

        return lax.map(per_time, jnp.arange(TSNK, dtype=jnp.int32))

    values = lax.map(per_source, jnp.arange(N_SRC, dtype=jnp.int32))
    starts = (jnp.cumsum(block_sizes) - block_sizes).astype(jnp.int32)
    offsets = jnp.arange(MAXB, dtype=jnp.int32)
    filled = offsets[None, :] < block_sizes[:, None]
    sink_times = jnp.where(filled, starts[:, None] + offsets[None, :], 0).astype(jnp.int32)
    picked = jnp.take(values, sink_times, axis=1)
    return picked * filled[None, :, :, None, None].astype(values.dtype)
```

```python
import functools

import jax
import jax.numpy as jnp
from jax import lax
from jax.experimental import pallas as pl
from jax.experimental.pallas import tpu as pltpu
from jax.sharding import PartitionSpec as P

NSN = 4
MAXB = 3


def slot_values(gathered, tau_slot, diagram_rows, phases):
    real_part = tau_slot[0]
    imag_part = tau_slot[1]
    left_stack = jnp.stack([jnp.stack([real_part, imag_part]), jnp.stack([-imag_part, real_part])])
    right_stack = jnp.stack([jnp.stack([real_part, -imag_part]), jnp.stack([imag_part, real_part])])
    left_node = lax.dot_general(
        gathered[:, :, :NSN],
        left_stack,
        (((1, 3), (0, 3)), ((), ())),
        preferred_element_type=jnp.float32,
    ).astype(jnp.bfloat16)
    right_node = lax.dot_general(
        gathered[:, :, NSN:],
        right_stack,
        (((1, 3), (0, 2)), ((), ())),
        preferred_element_type=jnp.float32,
    ).astype(jnp.bfloat16)
    pair_sums = lax.dot_general(
        left_node, right_node, (((0, 3), (3, 0)), ((), ())), preferred_element_type=jnp.float32
    )
    pair_real = pair_sums[:, 0, :, 0] - pair_sums[:, 1, :, 1]
    pair_imag = pair_sums[:, 0, :, 1] + pair_sums[:, 1, :, 0]
    sink_pick = (
        diagram_rows[:, 0:1] == jnp.arange(pair_real.shape[0], dtype=jnp.int32)[None, :]
    ).astype(jnp.float32)
    source_pick = (
        diagram_rows[:, 1:2] == jnp.arange(pair_real.shape[1], dtype=jnp.int32)[None, :]
    ).astype(jnp.float32)
    chosen_real = jnp.sum(
        sink_pick[:, :, None] * pair_real[None] * source_pick[:, None, :], axis=(1, 2)
    )
    chosen_imag = jnp.sum(
        sink_pick[:, :, None] * pair_imag[None] * source_pick[:, None, :], axis=(1, 2)
    )
    gamma_pick = diagram_rows[:, 2:3] == jnp.arange(phases.shape[0], dtype=jnp.int32)[None, :]
    quarter = jnp.sum(jnp.where(gamma_pick, phases[None, :], 0), axis=1)
    cosine = (quarter == 0).astype(jnp.float32) - (quarter == 2).astype(jnp.float32)
    sine_part = (quarter == 1).astype(jnp.float32) - (quarter == 3).astype(jnp.float32)
    return jnp.stack(
        [
            cosine * chosen_real - sine_part * chosen_imag,
            sine_part * chosen_real + cosine * chosen_imag,
        ]
    )


def plain_local(tau_cols, elementals, need_ids, diagrams, phases, block_sizes):
    groups = lax.axis_size("snk")
    column = lax.axis_index("snk")
    full_width = tau_cols.shape[4]
    col_count = tau_cols.shape[3]
    sink_count = tau_cols.shape[2]
    diagram_rows = diagrams[0]
    starts = jnp.cumsum(block_sizes) - block_sizes
    offsets = jnp.arange(MAXB, dtype=jnp.int32)
    picked = jnp.take(elementals, need_ids, axis=2)
    arrived = lax.all_to_all(picked, "src", split_axis=2, concat_axis=0, tiled=True)
    gathered = arrived.reshape(full_width, 2, need_ids.shape[1], full_width)
    local_tau = tau_cols[:, 0]
    per_group = sink_count // groups
    half_turn = groups // 2
    packed = local_tau.reshape(2, groups, per_group, col_count, full_width)
    packed = jnp.roll(packed, -half_turn, axis=1)
    arrived_tau = lax.all_to_all(packed, "snk", split_axis=1, concat_axis=3, tiled=True)
    blocks = arrived_tau.reshape(2, per_group, full_width, full_width)
    results = jnp.stack(
        [
            slot_values(gathered, blocks[:, place], diagram_rows, phases)
            for place in range(per_group)
        ]
    )
    all_values = lax.all_gather(results, "snk", axis=0, tiled=True)
    all_values = jnp.roll(all_values, half_turn * per_group, axis=0)
    own_start = lax.dynamic_index_in_dim(starts, column, keepdims=False)
    own_size = lax.dynamic_index_in_dim(block_sizes, column, keepdims=False)
    own_filled = offsets < own_size
    own_times = jnp.where(own_filled, own_start + offsets, 0)
    correlators = jnp.take(all_values, own_times, axis=0) * own_filled[:, None, None].astype(
        jnp.float32
    )
    return correlators.reshape(1, 1, MAXB, 2, diagram_rows.shape[0])


MESH = pl.DeviceIdType.MESH
SEND_ORDER = (4, 5, 6, 7, 2, 3, 1)
TAKE_ORDER = (0, 1, 4, 5, 2, 3, 6, 7)
NT = (((1,), (1,)), ((), ()))
NN = (((1,), (0,)), ((), ()))


def flipped(value, mask):
    for bit in (1, 2, 4):
        if mask & bit:
            value = value + bit * (1 - 2 * ((value // bit) % 2))
    return value


def kernel(
    ids_ref, diag_ref, phase_ref, size_ref, tau_ref, el_ref, out_ref,
    table, pick, sendbuf, ebuf, xbuf, xneg, lt, rt, vbuf,
    tab_sem, own_sem, tau_own, tau_send, tau_recv,
    src_send, src_recv, near_send, near_recv, far_send, far_recv, pass_send, pass_recv,
    val_send, val_recv,
):
    s = lax.axis_index("src")
    c = lax.axis_index("snk")
    x, h = c // 2, c % 2
    n_src, n_ids = ids_ref.shape
    rows, ne, nv = table.shape
    per = xbuf.shape[1]
    f32, bf16 = jnp.float32, jnp.bfloat16

    barrier = pltpu.get_barrier_semaphore()
    for m in range(1, n_src):
        pl.semaphore_signal(barrier, 1, device_id=(flipped(s, m), c), device_id_type=MESH)
    for m in range(1, 4):
        pl.semaphore_signal(barrier, 1, device_id=(s, flipped(c, m)), device_id_type=MESH)

    table_in = pltpu.make_async_copy(el_ref.at[pl.ds(h * rows, rows), x], table, tab_sem)
    table_in.start()
    tau_in = pltpu.make_async_copy(
        tau_ref.at[:, 0, pl.ds(c * per, per)], xbuf.at[:, :, c], tau_own
    )
    tau_in.start()

    sub = lax.broadcasted_iota(jnp.int32, (n_ids, ne), 0)
    lane = lax.broadcasted_iota(jnp.int32, (n_ids, ne), 1)
    hots = []
    for i in range(n_src):
        wanted = jnp.zeros((n_ids, ne), jnp.int32)
        for k in range(n_ids):
            wanted = jnp.where(sub == k, ids_ref[i, k], wanted)
        hots.append((wanted == lane).astype(f32))
    hot = jnp.concatenate(hots, axis=0).astype(bf16)

    pl.semaphore_wait(barrier, n_src - 1 + 3)
    tau_out = []
    for m in (2, 3, 1):
        peer = flipped(c, m)
        copy = pltpu.make_async_remote_copy(
            src_ref=tau_ref.at[:, 0, pl.ds(peer * per, per)], dst_ref=xbuf.at[:, :, c],
            send_sem=tau_send.at[m], recv_sem=tau_recv.at[m],
            device_id=(s, peer), device_id_type=MESH,
        )
        copy.start()
        tau_out.append(copy)

    table_in.wait()
    for r in range(rows):
        got = lax.dot_general(hot, table[r], NN, preferred_element_type=f32)
        for half in range(nv // 128):
            pick[half, pl.ds(r, n_src * n_ids, stride=rows), :] = got[:, half * 128:(half + 1) * 128]
    for i in range(n_src):
        for half in range(nv // 128):
            sendbuf[i, :, :, half * 128:(half + 1) * 128] = (
                pick[half, pl.ds(i * n_ids * rows, n_ids * rows), :]
                .astype(bf16)
                .reshape(n_ids, rows, 128)
            )

    def slot(source, column):
        return ebuf.at[column // 2, source * 2 + column % 2]

    src_out = {}
    for m in SEND_ORDER:
        peer = flipped(s, m)
        src_out[m] = pltpu.make_async_remote_copy(
            src_ref=sendbuf.at[peer], dst_ref=slot(s, c),
            send_sem=src_send.at[m], recv_sem=src_recv.at[m],
            device_id=(peer, c), device_id_type=MESH,
        )
        src_out[m].start()
    own = pltpu.make_async_copy(sendbuf.at[s], slot(s, c), own_sem)
    own.start()

    near, across = flipped(c, 1), flipped(c, 2)
    near_out, far_out, pass_out = {}, {}, {}

    def pass_on(m):
        far_out[m].wait_recv()
        came = slot(flipped(s, m), across)
        pass_out[m] = pltpu.make_async_remote_copy(
            src_ref=came, dst_ref=came,
            send_sem=pass_send.at[m], recv_sem=pass_recv.at[m],
            device_id=(s, near), device_id_type=MESH,
        )
        pass_out[m].start()

    for n, m in enumerate(TAKE_ORDER):
        mine = slot(flipped(s, m), c)
        if m == 0:
            own.wait()
        else:
            src_out[m].wait_recv()
        far_out[m] = pltpu.make_async_remote_copy(
            src_ref=mine, dst_ref=mine, send_sem=far_send.at[m], recv_sem=far_recv.at[m],
            device_id=(s, across), device_id_type=MESH,
        )
        far_out[m].start()
        near_out[m] = pltpu.make_async_remote_copy(
            src_ref=mine, dst_ref=mine, send_sem=near_send.at[m], recv_sem=near_recv.at[m],
            device_id=(s, near), device_id_type=MESH,
        )
        near_out[m].start()
        if n >= 1:
            pass_on(TAKE_ORDER[n - 1])
    pass_on(TAKE_ORDER[-1])

    tau_in.wait()
    for copy in tau_out:
        copy.wait_recv()
    for t in range(per):
        xneg[t] = -xbuf[1, t].reshape(nv, nv)
    for m in TAKE_ORDER:
        near_out[m].wait_recv()
        pass_out[m].wait_recv()

    def nodes(k, carry):
        left_re = ebuf[0, :, k].reshape(nv, nv)
        left_im = ebuf[1, :, k].reshape(nv, nv)
        right_re = ebuf[0, :, NSN + k].reshape(nv, nv)
        right_im = ebuf[1, :, NSN + k].reshape(nv, nv)
        for t in range(per):
            x_re = xbuf[0, t].reshape(nv, nv)
            x_im = xbuf[1, t].reshape(nv, nv)
            x_neg = xneg[t]

            def mm(a, b, dims):
                return lax.dot_general(a, b, dims, preferred_element_type=f32)

            def rounded(value):
                return value.astype(bf16).astype(f32)

            lt[k, t, 0] = rounded(mm(x_re, left_re, NT) + mm(x_neg, left_im, NT))
            lt[k, t, 1] = rounded(mm(x_re, left_im, NT) + mm(x_im, left_re, NT))
            rt[k, t, 0] = rounded(mm(right_re, x_re, NN) + mm(right_im, x_im, NN))
            rt[k, t, 1] = rounded(mm(right_im, x_re, NN) + mm(right_re, x_neg, NN))
        return carry

    lax.fori_loop(0, NSN, nodes, 0)

    n_diag = diag_ref.shape[1]
    picks = [(diag_ref[0, d, 0], diag_ref[0, d, 1], phase_ref[diag_ref[0, d, 2]]) for d in range(n_diag)]
    for t in range(per):

        def rows_of(block, sums):
            at = pl.ds(pl.multiple_of(block * 8, 8), 8)
            sums = list(sums)
            for half in range(nv // 128):
                lanes = slice(half * 128, (half + 1) * 128)
                for d, (k1, k2, _) in enumerate(picks):
                    a_re, a_im = lt[k1, t, 0, at, lanes], lt[k1, t, 1, at, lanes]
                    b_re, b_im = rt[k2, t, 0, at, lanes], rt[k2, t, 1, at, lanes]
                    sums[2 * d] = sums[2 * d] + a_re * b_re - a_im * b_im
                    sums[2 * d + 1] = sums[2 * d + 1] + a_re * b_im + a_im * b_re
            return tuple(sums)

        zero = jnp.zeros((8, 128), f32)
        sums = lax.fori_loop(0, nv // 8, rows_of, (zero,) * (2 * n_diag))
        real, imag = [], []
        for d, (_, _, turn) in enumerate(picks):
            cosine = (turn == 0).astype(f32) - (turn == 2).astype(f32)
            sine = (turn == 1).astype(f32) - (turn == 3).astype(f32)
            re = jnp.sum(sums[2 * d], axis=0, keepdims=True)
            im = jnp.sum(sums[2 * d + 1], axis=0, keepdims=True)
            real.append(cosine * re - sine * im)
            imag.append(sine * re + cosine * im)
        vbuf[c * per + t] = jnp.concatenate(real + imag, axis=0)

    val_out = []
    for m in (2, 3, 1):
        peer = flipped(c, m)
        mine = vbuf.at[pl.ds(c * per, per)]
        copy = pltpu.make_async_remote_copy(
            src_ref=mine, dst_ref=mine, send_sem=val_send.at[m], recv_sem=val_recv.at[m],
            device_id=(s, peer), device_id_type=MESH,
        )
        copy.start()
        val_out.append(copy)
    for copy in val_out:
        copy.wait_recv()

    first, size = 0, 0
    for j in range(size_ref.shape[0]):
        first = first + jnp.where(j < c, size_ref[j], 0)
        size = size + jnp.where(j == c, size_ref[j], 0)
    for place in range(MAXB):
        at = jnp.minimum(first + place, vbuf.shape[0] - 1)
        keep = (place < size).astype(f32)
        out_ref[place] = vbuf[at] * keep

    for m in TAKE_ORDER:
        if m:
            src_out[m].wait_send()
        far_out[m].wait_send()
        near_out[m].wait_send()
        pass_out[m].wait_send()
    for copy in tau_out + val_out:
        copy.wait_send()


def fused_local(tau_cols, elementals, need_ids, diagrams, phases, block_sizes):
    n_snk = lax.axis_size("snk")
    n_src, n_ids = need_ids.shape
    own_rows, _, ne, nv = elementals.shape
    sinks, cols = tau_cols.shape[2], tau_cols.shape[3]
    per = sinks // n_snk
    rows = own_rows // 2
    n_diag = diagrams.shape[1]
    bf16, f32 = jnp.bfloat16, jnp.float32
    sem = pltpu.SemaphoreType.DMA
    smem = pl.BlockSpec(memory_space=pltpu.SMEM)
    anywhere = pl.BlockSpec(memory_space=pl.ANY)
    partial = pl.pallas_call(
        kernel,
        out_shape=jax.ShapeDtypeStruct((MAXB, 2 * n_diag, 128), f32),
        in_specs=[smem] * 4 + [anywhere] * 2,
        out_specs=pl.BlockSpec(memory_space=pltpu.VMEM),
        scratch_shapes=[
            pltpu.VMEM((rows, ne, nv), bf16),
            pltpu.VMEM((nv // 128, n_src * n_ids * rows, 128), f32),
            pltpu.VMEM((n_src, n_ids, rows, nv), bf16),
            pltpu.VMEM((2, 2 * n_src, n_ids, rows, nv), bf16),
            pltpu.VMEM((2, per, n_snk, cols, nv), bf16),
            pltpu.VMEM((per, nv, nv), bf16),
            pltpu.VMEM((NSN, per, 2, nv, nv), f32),
            pltpu.VMEM((n_ids - NSN, per, 2, nv, nv), f32),
            pltpu.VMEM((sinks, 2 * n_diag, 128), f32),
            sem, sem, sem, sem((4,)), sem((4,)),
        ]
        + [sem((n_src,))] * 8
        + [sem((4,))] * 2,
        compiler_params=pltpu.CompilerParams(
            collective_id=0, has_side_effects=True, vmem_limit_bytes=50 * 1024 * 1024
        ),
    )(need_ids, diagrams, phases, block_sizes, tau_cols, elementals)
    return jnp.sum(partial, axis=2).reshape(1, 1, MAXB, 2, n_diag)


def local(tau_cols, elementals, *rest):
    fits = (
        lax.axis_size("snk") == 4
        and lax.axis_size("src") == 8
        and elementals.shape[0] == 32
        and tau_cols.shape[3] % 16 == 0
        and tau_cols.shape[4] % 128 == 0
    )
    return (fused_local if fits else plain_local)(tau_cols, elementals, *rest)


def solution(mesh):
    placed = (
        P(None, "src", None, "snk", None),
        P("src", None, None, None),
        P(),
        P("src", None, None),
        P(),
        P(),
    )
    return jax.shard_map(
        local,
        mesh=mesh,
        in_specs=placed,
        out_specs=P("src", "snk", None, None, None),
        check_vma=False,
    )
```

```python
import functools

import jax
import jax.numpy as jnp
from jax import lax
from jax.experimental import pallas as pl
from jax.experimental.pallas import tpu as pltpu
from jax.sharding import PartitionSpec as P

NSN = 4
MAXB = 3


def slot_values(gathered, tau_slot, diagram_rows, phases):
    real_part = tau_slot[0]
    imag_part = tau_slot[1]
    left_stack = jnp.stack([jnp.stack([real_part, imag_part]), jnp.stack([-imag_part, real_part])])
    right_stack = jnp.stack([jnp.stack([real_part, -imag_part]), jnp.stack([imag_part, real_part])])
    left_node = lax.dot_general(
        gathered[:, :, :NSN],
        left_stack,
        (((1, 3), (0, 3)), ((), ())),
        preferred_element_type=jnp.float32,
    ).astype(jnp.bfloat16)
    right_node = lax.dot_general(
        gathered[:, :, NSN:],
        right_stack,
        (((1, 3), (0, 2)), ((), ())),
        preferred_element_type=jnp.float32,
    ).astype(jnp.bfloat16)
    pair_sums = lax.dot_general(
        left_node, right_node, (((0, 3), (3, 0)), ((), ())), preferred_element_type=jnp.float32
    )
    pair_real = pair_sums[:, 0, :, 0] - pair_sums[:, 1, :, 1]
    pair_imag = pair_sums[:, 0, :, 1] + pair_sums[:, 1, :, 0]
    sink_pick = (
        diagram_rows[:, 0:1] == jnp.arange(pair_real.shape[0], dtype=jnp.int32)[None, :]
    ).astype(jnp.float32)
    source_pick = (
        diagram_rows[:, 1:2] == jnp.arange(pair_real.shape[1], dtype=jnp.int32)[None, :]
    ).astype(jnp.float32)
    chosen_real = jnp.sum(
        sink_pick[:, :, None] * pair_real[None] * source_pick[:, None, :], axis=(1, 2)
    )
    chosen_imag = jnp.sum(
        sink_pick[:, :, None] * pair_imag[None] * source_pick[:, None, :], axis=(1, 2)
    )
    gamma_pick = diagram_rows[:, 2:3] == jnp.arange(phases.shape[0], dtype=jnp.int32)[None, :]
    quarter = jnp.sum(jnp.where(gamma_pick, phases[None, :], 0), axis=1)
    cosine = (quarter == 0).astype(jnp.float32) - (quarter == 2).astype(jnp.float32)
    sine_part = (quarter == 1).astype(jnp.float32) - (quarter == 3).astype(jnp.float32)
    return jnp.stack(
        [
            cosine * chosen_real - sine_part * chosen_imag,
            sine_part * chosen_real + cosine * chosen_imag,
        ]
    )


def plain_local(tau_cols, elementals, need_ids, diagrams, phases, block_sizes):
    groups = lax.axis_size("snk")
    column = lax.axis_index("snk")
    full_width = tau_cols.shape[4]
    col_count = tau_cols.shape[3]
    sink_count = tau_cols.shape[2]
    diagram_rows = diagrams[0]
    starts = jnp.cumsum(block_sizes) - block_sizes
    offsets = jnp.arange(MAXB, dtype=jnp.int32)
    picked = jnp.take(elementals, need_ids, axis=2)
    arrived = lax.all_to_all(picked, "src", split_axis=2, concat_axis=0, tiled=True)
    gathered = arrived.reshape(full_width, 2, need_ids.shape[1], full_width)
    local_tau = tau_cols[:, 0]
    per_group = sink_count // groups
    half_turn = groups // 2
    packed = local_tau.reshape(2, groups, per_group, col_count, full_width)
    packed = jnp.roll(packed, -half_turn, axis=1)
    arrived_tau = lax.all_to_all(packed, "snk", split_axis=1, concat_axis=3, tiled=True)
    blocks = arrived_tau.reshape(2, per_group, full_width, full_width)
    results = jnp.stack(
        [
            slot_values(gathered, blocks[:, place], diagram_rows, phases)
            for place in range(per_group)
        ]
    )
    all_values = lax.all_gather(results, "snk", axis=0, tiled=True)
    all_values = jnp.roll(all_values, half_turn * per_group, axis=0)
    own_start = lax.dynamic_index_in_dim(starts, column, keepdims=False)
    own_size = lax.dynamic_index_in_dim(block_sizes, column, keepdims=False)
    own_filled = offsets < own_size
    own_times = jnp.where(own_filled, own_start + offsets, 0)
    correlators = jnp.take(all_values, own_times, axis=0) * own_filled[:, None, None].astype(
        jnp.float32
    )
    return correlators.reshape(1, 1, MAXB, 2, diagram_rows.shape[0])


MESH = pl.DeviceIdType.MESH
HALF = 4
RELAYED = (4, 5, 6, 7)
DIRECT = (2, 3, 1)
NT = (((1,), (1,)), ((), ()))
NN = (((1,), (0,)), ((), ()))


def flipped(value, mask):
    for bit in (1, 2, 4):
        if mask & bit:
            value = value + bit * (1 - 2 * ((value // bit) % 2))
    return value


def kernel(
    ids_hbm, diag_hbm, phase_hbm, size_hbm, tau_ref, el_ref, out_ref,
    ids_ref, diag_ref, phase_ref, size_ref,
    table, pick, sendbuf, sendother, ebuf, xbuf, xneg, lt, rt, vbuf,
    small_sem, tab_sem, own_sem, tau_own, tau_send, tau_recv,
    src_send, src_recv, near_send, near_recv, far_send, far_recv,
    val_send, val_recv,
):
    s = lax.axis_index("src")
    c = lax.axis_index("snk")
    x, h = c // 2, c % 2
    n_src, n_ids = ids_ref.shape
    rows, ne, nv = table.shape[1:]
    per = xbuf.shape[1]
    f32, bf16 = jnp.float32, jnp.bfloat16
    base = (s // HALF) * HALF

    smalls = []
    for n, (there, here) in enumerate(
        ((ids_hbm, ids_ref), (diag_hbm, diag_ref), (phase_hbm, phase_ref), (size_hbm, size_ref))
    ):
        smalls.append(pltpu.make_async_copy(there, here, small_sem.at[n]))
        smalls[-1].start()
    table_in = []
    for n, part in enumerate((x, 1 - x)):
        table_in.append(
            pltpu.make_async_copy(el_ref.at[pl.ds(h * rows, rows), part], table.at[n], tab_sem.at[n])
        )
        table_in[-1].start()

    barrier = pltpu.get_barrier_semaphore()
    for m in range(1, n_src):
        pl.semaphore_signal(barrier, 1, device_id=(flipped(s, m), c), device_id_type=MESH)
    for m in range(1, 4):
        pl.semaphore_signal(barrier, 1, device_id=(s, flipped(c, m)), device_id_type=MESH)

    tau_in = pltpu.make_async_copy(
        tau_ref.at[:, 0, pl.ds(c * per, per)], xbuf.at[:, :, c], tau_own
    )
    tau_in.start()

    sub = lax.broadcasted_iota(jnp.int32, (n_ids, ne), 0)
    lane = lax.broadcasted_iota(jnp.int32, (n_ids, ne), 1)
    smalls[0].wait()

    def one_hot(owners):
        hots = []
        for i in owners:
            wanted = jnp.zeros((n_ids, ne), jnp.int32)
            for k in range(n_ids):
                wanted = jnp.where(sub == k, ids_ref[i, k], wanted)
            hots.append((wanted == lane).astype(f32))
        return jnp.concatenate(hots, axis=0).astype(bf16)

    def pick_rows(n, hot, target):
        count = target.shape[0] * n_ids
        for r in range(rows):
            got = lax.dot_general(hot, table[n, r], NN, preferred_element_type=f32)
            for half in range(nv // 128):
                pick[half, pl.ds(r, count, stride=rows), :] = got[:, half * 128:(half + 1) * 128]
        for i in range(target.shape[0]):
            for half in range(nv // 128):
                target[i, :, :, half * 128:(half + 1) * 128] = (
                    pick[half, pl.ds(i * n_ids * rows, n_ids * rows), :]
                    .astype(bf16)
                    .reshape(n_ids, rows, 128)
                )

    hot = one_hot(range(n_src))
    pl.semaphore_wait(barrier, n_src - 1 + 3)
    tau_out = []
    for m in (2, 3, 1):
        peer = flipped(c, m)
        copy = pltpu.make_async_remote_copy(
            src_ref=tau_ref.at[:, 0, pl.ds(peer * per, per)], dst_ref=xbuf.at[:, :, c],
            send_sem=tau_send.at[m], recv_sem=tau_recv.at[m],
            device_id=(s, peer), device_id_type=MESH,
        )
        copy.start()
        tau_out.append(copy)

    def slot(part, source):
        return ebuf.at[part, source * 2 + h]

    src_out = {}

    def send_on(n, m, chunk):
        src_out[n, m] = pltpu.make_async_remote_copy(
            src_ref=chunk, dst_ref=slot((x, 1 - x)[n], s),
            send_sem=src_send.at[n, m], recv_sem=src_recv.at[n, m],
            device_id=(flipped(s, m), c), device_id_type=MESH,
        )
        src_out[n, m].start()

    table_in[0].wait()
    pick_rows(0, hot, sendbuf)
    for m in RELAYED + DIRECT:
        send_on(0, m, sendbuf.at[flipped(s, m)])
    own = [pltpu.make_async_copy(sendbuf.at[s], slot(x, s), own_sem.at[0])]
    own[0].start()
    table_in[1].wait()
    pick_rows(1, one_hot([base + i for i in range(HALF)]), sendother)
    for m in DIRECT:
        send_on(1, m, sendother.at[flipped(s, m) - base])
    own.append(pltpu.make_async_copy(sendother.at[s - base], slot(1 - x, s), own_sem.at[1]))
    own[1].start()

    near, across = flipped(c, 1), flipped(c, 2)
    near_out, far_out = {}, {}

    def to_near(n, m):
        chunk = slot((x, 1 - x)[n], flipped(s, m))
        near_out[n, m] = pltpu.make_async_remote_copy(
            src_ref=chunk, dst_ref=chunk, send_sem=near_send.at[n, m], recv_sem=near_recv.at[n, m],
            device_id=(s, near), device_id_type=MESH,
        )
        near_out[n, m].start()

    for n in (0, 1):
        own[n].wait()
        to_near(n, 0)
    for n in (0, 1):
        src_out[n, 1].wait_recv()
        to_near(n, 1)
    for m in RELAYED:
        src_out[0, m].wait_recv()
        chunk = slot(x, flipped(s, m))
        far_out[m] = pltpu.make_async_remote_copy(
            src_ref=chunk, dst_ref=chunk, send_sem=far_send.at[m], recv_sem=far_recv.at[m],
            device_id=(s, across), device_id_type=MESH,
        )
        far_out[m].start()
        to_near(0, m)
    for m in (2, 3):
        for n in (0, 1):
            src_out[n, m].wait_recv()
            to_near(n, m)
    for m in RELAYED:
        far_out[m].wait_recv()
        to_near(1, m)

    tau_in.wait()
    for copy in tau_out:
        copy.wait_recv()
    for t in range(per):
        xneg[t] = -xbuf[1, t].reshape(nv, nv)
    for copy in near_out.values():
        copy.wait_recv()

    def nodes(k, carry):
        left_re = ebuf[0, :, k].reshape(nv, nv)
        left_im = ebuf[1, :, k].reshape(nv, nv)
        right_re = ebuf[0, :, NSN + k].reshape(nv, nv)
        right_im = ebuf[1, :, NSN + k].reshape(nv, nv)
        for t in range(per):
            x_re = xbuf[0, t].reshape(nv, nv)
            x_im = xbuf[1, t].reshape(nv, nv)
            x_neg = xneg[t]

            def mm(a, b, dims):
                return lax.dot_general(a, b, dims, preferred_element_type=f32)

            def rounded(value):
                return value.astype(bf16).astype(f32)

            lt[k, t, 0] = rounded(mm(x_re, left_re, NT) + mm(x_neg, left_im, NT))
            lt[k, t, 1] = rounded(mm(x_re, left_im, NT) + mm(x_im, left_re, NT))
            rt[k, t, 0] = rounded(mm(right_re, x_re, NN) + mm(right_im, x_im, NN))
            rt[k, t, 1] = rounded(mm(right_im, x_re, NN) + mm(right_re, x_neg, NN))
        return carry

    lax.fori_loop(0, NSN, nodes, 0)

    n_diag = diag_ref.shape[2]
    for copy in smalls[1:]:
        copy.wait()
    picks = [(diag_ref[0, 0, d], diag_ref[1, 0, d], phase_ref[diag_ref[2, 0, d]]) for d in range(n_diag)]
    for t in range(per):

        def rows_of(block, sums):
            at = pl.ds(pl.multiple_of(block * 8, 8), 8)
            sums = list(sums)
            for half in range(nv // 128):
                lanes = slice(half * 128, (half + 1) * 128)
                for d, (k1, k2, _) in enumerate(picks):
                    a_re, a_im = lt[k1, t, 0, at, lanes], lt[k1, t, 1, at, lanes]
                    b_re, b_im = rt[k2, t, 0, at, lanes], rt[k2, t, 1, at, lanes]
                    sums[2 * d] = sums[2 * d] + a_re * b_re - a_im * b_im
                    sums[2 * d + 1] = sums[2 * d + 1] + a_re * b_im + a_im * b_re
            return tuple(sums)

        zero = jnp.zeros((8, 128), f32)
        sums = lax.fori_loop(0, nv // 8, rows_of, (zero,) * (2 * n_diag))
        real, imag = [], []
        for d, (_, _, turn) in enumerate(picks):
            cosine = (turn == 0).astype(f32) - (turn == 2).astype(f32)
            sine = (turn == 1).astype(f32) - (turn == 3).astype(f32)
            re = jnp.sum(sums[2 * d], axis=0, keepdims=True)
            im = jnp.sum(sums[2 * d + 1], axis=0, keepdims=True)
            real.append(cosine * re - sine * im)
            imag.append(sine * re + cosine * im)
        vbuf[c * per + t] = jnp.concatenate(real + imag, axis=0)

    val_out = []
    for m in (2, 3, 1):
        peer = flipped(c, m)
        mine = vbuf.at[pl.ds(c * per, per)]
        copy = pltpu.make_async_remote_copy(
            src_ref=mine, dst_ref=mine, send_sem=val_send.at[m], recv_sem=val_recv.at[m],
            device_id=(s, peer), device_id_type=MESH,
        )
        copy.start()
        val_out.append(copy)
    for copy in val_out:
        copy.wait_recv()

    first, size = 0, 0
    for j in range(size_ref.shape[0]):
        first = first + jnp.where(j < c, size_ref[j], 0)
        size = size + jnp.where(j == c, size_ref[j], 0)
    for place in range(MAXB):
        at = jnp.minimum(first + place, vbuf.shape[0] - 1)
        keep = (place < size).astype(f32)
        out_ref[place] = vbuf[at] * keep

    for copy in list(src_out.values()) + list(far_out.values()) + list(near_out.values()):
        copy.wait_send()
    for copy in tau_out + val_out:
        copy.wait_send()


def fused_local(tau_cols, elementals, need_ids, diagrams, phases, block_sizes):
    n_snk = lax.axis_size("snk")
    n_src, n_ids = need_ids.shape
    own_rows, _, ne, nv = elementals.shape
    sinks, cols = tau_cols.shape[2], tau_cols.shape[3]
    per = sinks // n_snk
    rows = own_rows // 2
    n_diag = diagrams.shape[1]
    bf16, f32 = jnp.bfloat16, jnp.float32
    sem = pltpu.SemaphoreType.DMA
    i32 = jnp.int32
    held = pl.BlockSpec(memory_space=pltpu.HBM)
    partial = pl.pallas_call(
        kernel,
        out_shape=jax.ShapeDtypeStruct((MAXB, 2 * n_diag, 128), f32),
        in_specs=[held] * 6,
        out_specs=pl.BlockSpec(memory_space=pltpu.VMEM),
        scratch_shapes=[
            pltpu.SMEM((n_src, n_ids), i32),
            pltpu.SMEM((3, 1, n_diag), i32),
            pltpu.SMEM(phases.shape, i32),
            pltpu.SMEM(block_sizes.shape, i32),
            pltpu.VMEM((2, rows, ne, nv), bf16),
            pltpu.VMEM((nv // 128, n_src * n_ids * rows, 128), f32),
            pltpu.VMEM((n_src, n_ids, rows, nv), bf16),
            pltpu.VMEM((HALF, n_ids, rows, nv), bf16),
            pltpu.VMEM((2, 2 * n_src, n_ids, rows, nv), bf16),
            pltpu.VMEM((2, per, n_snk, cols, nv), bf16),
            pltpu.VMEM((per, nv, nv), bf16),
            pltpu.VMEM((NSN, per, 2, nv, nv), f32),
            pltpu.VMEM((n_ids - NSN, per, 2, nv, nv), f32),
            pltpu.VMEM((sinks, 2 * n_diag, 128), f32),
            sem((4,)), sem((2,)), sem((2,)), sem, sem((4,)), sem((4,)),
        ]
        + [sem((2, n_src))] * 4
        + [sem((n_src,))] * 2
        + [sem((4,))] * 2,
        compiler_params=pltpu.CompilerParams(
            collective_id=0, has_side_effects=True, vmem_limit_bytes=67043328
        ),
    )(need_ids, jnp.transpose(diagrams, (2, 0, 1)), phases, block_sizes, tau_cols, elementals)
    return jnp.sum(partial, axis=2).reshape(1, 1, MAXB, 2, n_diag)


def local(tau_cols, elementals, *rest):
    fits = (
        lax.axis_size("snk") == 4
        and lax.axis_size("src") == 8
        and elementals.shape[0] == 32
        and tau_cols.shape[3] % 16 == 0
        and tau_cols.shape[4] % 128 == 0
    )
    return (fused_local if fits else plain_local)(tau_cols, elementals, *rest)


def solution(mesh):
    placed = (
        P(None, "src", None, "snk", None),
        P("src", None, None, None),
        P(),
        P("src", None, None),
        P(),
        P(),
    )
    return jax.shard_map(
        local,
        mesh=mesh,
        in_specs=placed,
        out_specs=P("src", "snk", None, None, None),
        check_vma=False,
    )
```

```python
import functools

import jax
import jax.numpy as jnp
from jax import lax
from jax.experimental import pallas as pl
from jax.experimental.pallas import tpu as pltpu
from jax.sharding import PartitionSpec as P

NSN = 4
MAXB = 3


def slot_values(gathered, tau_slot, diagram_rows, phases):
    real_part = tau_slot[0]
    imag_part = tau_slot[1]
    left_stack = jnp.stack([jnp.stack([real_part, imag_part]), jnp.stack([-imag_part, real_part])])
    right_stack = jnp.stack([jnp.stack([real_part, -imag_part]), jnp.stack([imag_part, real_part])])
    left_node = lax.dot_general(
        gathered[:, :, :NSN],
        left_stack,
        (((1, 3), (0, 3)), ((), ())),
        preferred_element_type=jnp.float32,
    ).astype(jnp.bfloat16)
    right_node = lax.dot_general(
        gathered[:, :, NSN:],
        right_stack,
        (((1, 3), (0, 2)), ((), ())),
        preferred_element_type=jnp.float32,
    ).astype(jnp.bfloat16)
    pair_sums = lax.dot_general(
        left_node, right_node, (((0, 3), (3, 0)), ((), ())), preferred_element_type=jnp.float32
    )
    pair_real = pair_sums[:, 0, :, 0] - pair_sums[:, 1, :, 1]
    pair_imag = pair_sums[:, 0, :, 1] + pair_sums[:, 1, :, 0]
    sink_pick = (
        diagram_rows[:, 0:1] == jnp.arange(pair_real.shape[0], dtype=jnp.int32)[None, :]
    ).astype(jnp.float32)
    source_pick = (
        diagram_rows[:, 1:2] == jnp.arange(pair_real.shape[1], dtype=jnp.int32)[None, :]
    ).astype(jnp.float32)
    chosen_real = jnp.sum(
        sink_pick[:, :, None] * pair_real[None] * source_pick[:, None, :], axis=(1, 2)
    )
    chosen_imag = jnp.sum(
        sink_pick[:, :, None] * pair_imag[None] * source_pick[:, None, :], axis=(1, 2)
    )
    gamma_pick = diagram_rows[:, 2:3] == jnp.arange(phases.shape[0], dtype=jnp.int32)[None, :]
    quarter = jnp.sum(jnp.where(gamma_pick, phases[None, :], 0), axis=1)
    cosine = (quarter == 0).astype(jnp.float32) - (quarter == 2).astype(jnp.float32)
    sine_part = (quarter == 1).astype(jnp.float32) - (quarter == 3).astype(jnp.float32)
    return jnp.stack(
        [
            cosine * chosen_real - sine_part * chosen_imag,
            sine_part * chosen_real + cosine * chosen_imag,
        ]
    )


def plain_local(tau_cols, elementals, need_ids, diagrams, phases, block_sizes):
    groups = lax.axis_size("snk")
    column = lax.axis_index("snk")
    full_width = tau_cols.shape[4]
    col_count = tau_cols.shape[3]
    sink_count = tau_cols.shape[2]
    diagram_rows = diagrams[0]
    starts = jnp.cumsum(block_sizes) - block_sizes
    offsets = jnp.arange(MAXB, dtype=jnp.int32)
    picked = jnp.take(elementals, need_ids, axis=2)
    arrived = lax.all_to_all(picked, "src", split_axis=2, concat_axis=0, tiled=True)
    gathered = arrived.reshape(full_width, 2, need_ids.shape[1], full_width)
    local_tau = tau_cols[:, 0]
    per_group = sink_count // groups
    half_turn = groups // 2
    packed = local_tau.reshape(2, groups, per_group, col_count, full_width)
    packed = jnp.roll(packed, -half_turn, axis=1)
    arrived_tau = lax.all_to_all(packed, "snk", split_axis=1, concat_axis=3, tiled=True)
    blocks = arrived_tau.reshape(2, per_group, full_width, full_width)
    results = jnp.stack(
        [
            slot_values(gathered, blocks[:, place], diagram_rows, phases)
            for place in range(per_group)
        ]
    )
    all_values = lax.all_gather(results, "snk", axis=0, tiled=True)
    all_values = jnp.roll(all_values, half_turn * per_group, axis=0)
    own_start = lax.dynamic_index_in_dim(starts, column, keepdims=False)
    own_size = lax.dynamic_index_in_dim(block_sizes, column, keepdims=False)
    own_filled = offsets < own_size
    own_times = jnp.where(own_filled, own_start + offsets, 0)
    correlators = jnp.take(all_values, own_times, axis=0) * own_filled[:, None, None].astype(
        jnp.float32
    )
    return correlators.reshape(1, 1, MAXB, 2, diagram_rows.shape[0])


MESH = pl.DeviceIdType.MESH
HALF = 4
DIRECT = (2, 3, 1)
NT = (((1,), (1,)), ((), ()))
NN = (((1,), (0,)), ((), ()))


def flipped(value, mask):
    for bit in (1, 2, 4):
        if mask & bit:
            value = value + bit * (1 - 2 * ((value // bit) % 2))
    return value


def kernel(
    ids_hbm, diag_hbm, phase_hbm, size_hbm, tau_ref, el_ref, out_ref,
    ids_ref, diag_ref, phase_ref, size_ref,
    table, pick, sendbuf, sendother, ebuf, xbuf, xneg, lt, rt, vbuf,
    small_sem, tab_sem, own_sem, tau_own, tau_send, tau_recv,
    src_send, src_recv, near_send, near_recv, far_send, far_recv,
    val_send, val_recv,
):
    s = lax.axis_index("src")
    c = lax.axis_index("snk")
    x, h = c // 2, c % 2
    n_src, n_ids = ids_ref.shape
    rows, ne, nv = table.shape[1:]
    per = xbuf.shape[1]
    f32, bf16 = jnp.float32, jnp.bfloat16
    base = (s // HALF) * HALF

    smalls = []
    for n, (there, here) in enumerate(
        ((ids_hbm, ids_ref), (diag_hbm, diag_ref), (phase_hbm, phase_ref), (size_hbm, size_ref))
    ):
        smalls.append(pltpu.make_async_copy(there, here, small_sem.at[n]))
        smalls[-1].start()
    table_in = []
    for n, part in enumerate((x, 1 - x)):
        table_in.append(
            pltpu.make_async_copy(el_ref.at[pl.ds(h * rows, rows), part], table.at[n], tab_sem.at[n])
        )
        table_in[-1].start()

    barrier = pltpu.get_barrier_semaphore()
    for m in range(1, n_src):
        pl.semaphore_signal(barrier, 1, device_id=(flipped(s, m), c), device_id_type=MESH)
    for m in range(1, 4):
        pl.semaphore_signal(barrier, 1, device_id=(s, flipped(c, m)), device_id_type=MESH)

    tau_in = pltpu.make_async_copy(
        tau_ref.at[:, 0, pl.ds(c * per, per)], xbuf.at[:, :, c], tau_own
    )
    tau_in.start()

    sub = lax.broadcasted_iota(jnp.int32, (n_ids, ne), 0)
    lane = lax.broadcasted_iota(jnp.int32, (n_ids, ne), 1)
    smalls[0].wait()

    def one_hot(owners):
        hots = []
        for i in owners:
            wanted = jnp.zeros((n_ids, ne), jnp.int32)
            for k in range(n_ids):
                wanted = jnp.where(sub == k, ids_ref[i, k], wanted)
            hots.append((wanted == lane).astype(f32))
        return jnp.concatenate(hots, axis=0).astype(bf16)

    def pick_rows(n, hot, target):
        count = target.shape[0] * n_ids
        for r in range(rows):
            got = lax.dot_general(hot, table[n, r], NN, preferred_element_type=f32)
            for half in range(nv // 128):
                pick[half, pl.ds(r, count, stride=rows), :] = got[:, half * 128:(half + 1) * 128]
        for i in range(target.shape[0]):
            for half in range(nv // 128):
                target[i, :, :, half * 128:(half + 1) * 128] = (
                    pick[half, pl.ds(i * n_ids * rows, n_ids * rows), :]
                    .astype(bf16)
                    .reshape(n_ids, rows, 128)
                )

    hot = one_hot(range(n_src))
    pl.semaphore_wait(barrier, n_src - 1 + 3)
    tau_out = []
    for m in (2, 3, 1):
        peer = flipped(c, m)
        copy = pltpu.make_async_remote_copy(
            src_ref=tau_ref.at[:, 0, pl.ds(peer * per, per)], dst_ref=xbuf.at[:, :, c],
            send_sem=tau_send.at[m], recv_sem=tau_recv.at[m],
            device_id=(s, peer), device_id_type=MESH,
        )
        copy.start()
        tau_out.append(copy)

    def slot(part, source):
        return ebuf.at[part, source * 2 + h]

    src_out = {}
    depth, lane_y = s // 2, s % 2
    inner = ((depth + 1) // 2) % 2
    other_half = 1 - depth // 2
    inner_at, outer_at = 1 + other_half, 3 * other_half

    def send_on(n, m, chunk):
        src_out[n, m] = pltpu.make_async_remote_copy(
            src_ref=chunk, dst_ref=slot((x, 1 - x)[n], s),
            send_sem=src_send.at[n, m], recv_sem=src_recv.at[n, m],
            device_id=(flipped(s, m), c), device_id_type=MESH,
        )
        src_out[n, m].start()

    across_out = []
    for n, there in enumerate((inner_at, outer_at)):
        for y_flip in (0, 1):
            peer = there * 2 + flipped(lane_y, y_flip)
            across_out.append(
                pltpu.make_async_remote_copy(
                    src_ref=sendbuf.at[peer], dst_ref=slot(x, s),
                    send_sem=src_send.at[0, HALF + 2 * n + y_flip],
                    recv_sem=src_recv.at[0, HALF + 2 * (1 - inner) + y_flip],
                    device_id=(peer, c), device_id_type=MESH,
                )
            )

    table_in[0].wait()
    pick_rows(0, hot, sendbuf)

    @pl.when(inner == 1)
    def _():
        for copy in across_out:
            copy.start()

    for m in DIRECT:
        send_on(0, m, sendbuf.at[flipped(s, m)])
    own = [pltpu.make_async_copy(sendbuf.at[s], slot(x, s), own_sem.at[0])]
    own[0].start()
    table_in[1].wait()
    pick_rows(1, one_hot([base + i for i in range(HALF)]), sendother)
    for m in DIRECT:
        send_on(1, m, sendother.at[flipped(s, m) - base])
    own.append(pltpu.make_async_copy(sendother.at[s - base], slot(1 - x, s), own_sem.at[1]))
    own[1].start()

    @pl.when(inner == 0)
    def _():
        for copy in across_out:
            copy.start()

    near, across = flipped(c, 1), flipped(c, 2)
    near_out, far_out = {}, {}

    def to_near(n, m, source):
        chunk = slot((x, 1 - x)[n], source)
        near_out[n, m] = pltpu.make_async_remote_copy(
            src_ref=chunk, dst_ref=chunk, send_sem=near_send.at[n, m], recv_sem=near_recv.at[n, m],
            device_id=(s, near), device_id_type=MESH,
        )
        near_out[n, m].start()

    def relayed_from(q):
        return (inner_at, outer_at)[q // 2] * 2 + flipped(lane_y, q % 2)

    def relay(q):
        chunk = slot(x, relayed_from(q))
        far_out[q] = pltpu.make_async_remote_copy(
            src_ref=chunk, dst_ref=chunk, send_sem=far_send.at[q], recv_sem=far_recv.at[q],
            device_id=(s, across), device_id_type=MESH,
        )
        pltpu.make_async_remote_copy(
            src_ref=chunk, dst_ref=chunk, send_sem=far_send.at[q], recv_sem=src_recv.at[0, HALF + q],
            device_id=(s, across), device_id_type=MESH,
        ).wait_recv()
        far_out[q].start()
        to_near(0, HALF + q, relayed_from(q))

    for n in (0, 1):
        own[n].wait()
        to_near(n, 0, s)
    for m in (1, 2):
        src_out[0, m].wait_recv()
        to_near(0, m, flipped(s, m))
    relay(0)
    src_out[0, 3].wait_recv()
    to_near(0, 3, flipped(s, 3))
    relay(1)
    for m in (1, 2, 3):
        src_out[1, m].wait_recv()
        to_near(1, m, flipped(s, m))

    tau_in.wait()
    for copy in tau_out:
        copy.wait_recv()
    for t in range(per):
        xneg[t] = -xbuf[1, t].reshape(nv, nv)
    for n in (0, 1):
        for m in range(HALF):
            near_out[n, m].wait_recv()

    part_rows = nv // 2
    blocks = part_rows // rows

    def mm(a, b, dims):
        return lax.dot_general(a, b, dims, preferred_element_type=f32)

    def rounded(value):
        return value.astype(bf16).astype(f32)

    def nodes(side):
        at = pl.ds(side * blocks, blocks)

        def stacked(part, first, count):
            return jnp.concatenate(
                [ebuf[part, at, first + k].reshape(part_rows, nv) for k in range(count)], axis=0
            )

        def left_pair(j, carry):
            left_re, left_im = stacked(0, 2 * j, 2), stacked(1, 2 * j, 2)
            for t in range(per):
                x_re, x_im = xbuf[0, t].reshape(nv, nv), xbuf[1, t].reshape(nv, nv)
                re = rounded(mm(x_re, left_re, NT) + mm(xneg[t], left_im, NT))
                im = rounded(mm(x_re, left_im, NT) + mm(x_im, left_re, NT))
                for k in range(2):
                    lanes = slice(k * part_rows, (k + 1) * part_rows)
                    lt[2 * j + k, t, 0, side] = re[:, lanes]
                    lt[2 * j + k, t, 1, side] = im[:, lanes]
            return carry

        lax.fori_loop(0, NSN // 2, left_pair, 0)

        def right_time(t, carry):
            x_re, x_im, x_neg = xbuf[0, t].reshape(nv, nv), xbuf[1, t].reshape(nv, nv), xneg[t]
            for j in range((n_ids - NSN) // 2):
                right_re, right_im = stacked(0, NSN + 2 * j, 2), stacked(1, NSN + 2 * j, 2)
                re = rounded(mm(right_re, x_re, NN) + mm(right_im, x_im, NN))
                im = rounded(mm(right_im, x_re, NN) + mm(right_re, x_neg, NN))
                for k in range(2):
                    down = slice(k * part_rows, (k + 1) * part_rows)
                    for half in range(2):
                        lanes = slice(half * part_rows, (half + 1) * part_rows)
                        rt[2 * j + k, t, 0, side, half] = re[down, lanes]
                        rt[2 * j + k, t, 1, side, half] = im[down, lanes]
            return carry

        lax.fori_loop(0, per, right_time, 0)

    n_diag = diag_ref.shape[2]
    for copy in smalls[1:]:
        copy.wait()
    picks = [(diag_ref[0, 0, d], diag_ref[1, 0, d], phase_ref[diag_ref[2, 0, d]]) for d in range(n_diag)]

    def products(t, down, acrosses, sums):
        def rows_of(block, sums):
            at = pl.ds(pl.multiple_of(block * 8, 8), 8)
            left_at = pl.ds(pl.multiple_of(down * part_rows + block * 8, 8), 8)
            sums = list(sums)
            for half in acrosses:
                for d, (k1, k2, _) in enumerate(picks):
                    a_re, a_im = lt[k1, t, 0, half, left_at, :], lt[k1, t, 1, half, left_at, :]
                    b_re, b_im = rt[k2, t, 0, down, half, at, :], rt[k2, t, 1, down, half, at, :]
                    sums[2 * d] = sums[2 * d] + a_re * b_re - a_im * b_im
                    sums[2 * d + 1] = sums[2 * d + 1] + a_re * b_im + a_im * b_re
            return tuple(sums)

        return lax.fori_loop(0, part_rows // 8, rows_of, sums)

    zero = jnp.zeros((8, 128), f32)
    here, there = depth // 2, other_half
    def pass_on(q):
        far_out[q].wait_recv()
        to_near(1, HALF + q, relayed_from(q))

    relay(2)
    pass_on(0)
    nodes(here)
    relay(3)
    pass_on(1)
    pass_on(2)
    early = [products(t, here, (here,), (zero,) * (2 * n_diag)) for t in range(per)]
    pass_on(3)
    for n in (0, 1):
        for q in range(4):
            near_out[n, HALF + q].wait_recv()
    nodes(there)
    for t in range(per):
        sums = products(t, here, (there,), early[t])
        sums = products(t, there, (here, there), sums)
        real, imag = [], []
        for d, (_, _, turn) in enumerate(picks):
            cosine = (turn == 0).astype(f32) - (turn == 2).astype(f32)
            sine = (turn == 1).astype(f32) - (turn == 3).astype(f32)
            re = jnp.sum(sums[2 * d], axis=0, keepdims=True)
            im = jnp.sum(sums[2 * d + 1], axis=0, keepdims=True)
            real.append(cosine * re - sine * im)
            imag.append(sine * re + cosine * im)
        vbuf[c * per + t] = jnp.concatenate(real + imag, axis=0)

    val_out = []
    for m in (2, 3, 1):
        peer = flipped(c, m)
        mine = vbuf.at[pl.ds(c * per, per)]
        copy = pltpu.make_async_remote_copy(
            src_ref=mine, dst_ref=mine, send_sem=val_send.at[m], recv_sem=val_recv.at[m],
            device_id=(s, peer), device_id_type=MESH,
        )
        copy.start()
        val_out.append(copy)
    for copy in val_out:
        copy.wait_recv()

    first, size = 0, 0
    for j in range(size_ref.shape[0]):
        first = first + jnp.where(j < c, size_ref[j], 0)
        size = size + jnp.where(j == c, size_ref[j], 0)
    for place in range(MAXB):
        at = jnp.minimum(first + place, vbuf.shape[0] - 1)
        keep = (place < size).astype(f32)
        out_ref[place] = vbuf[at] * keep

    for copy in list(src_out.values()) + across_out + list(far_out.values()) + list(near_out.values()):
        copy.wait_send()
    for copy in tau_out + val_out:
        copy.wait_send()


def fused_local(tau_cols, elementals, need_ids, diagrams, phases, block_sizes):
    n_snk = lax.axis_size("snk")
    n_src, n_ids = need_ids.shape
    own_rows, _, ne, nv = elementals.shape
    sinks, cols = tau_cols.shape[2], tau_cols.shape[3]
    per = sinks // n_snk
    rows = own_rows // 2
    n_diag = diagrams.shape[1]
    bf16, f32 = jnp.bfloat16, jnp.float32
    sem = pltpu.SemaphoreType.DMA
    i32 = jnp.int32
    held = pl.BlockSpec(memory_space=pltpu.HBM)
    partial = pl.pallas_call(
        kernel,
        out_shape=jax.ShapeDtypeStruct((MAXB, 2 * n_diag, 128), f32),
        in_specs=[held] * 6,
        out_specs=pl.BlockSpec(memory_space=pltpu.VMEM),
        scratch_shapes=[
            pltpu.SMEM((n_src, n_ids), i32),
            pltpu.SMEM((3, 1, n_diag), i32),
            pltpu.SMEM(phases.shape, i32),
            pltpu.SMEM(block_sizes.shape, i32),
            pltpu.VMEM((2, rows, ne, nv), bf16),
            pltpu.VMEM((nv // 128, n_src * n_ids * rows, 128), f32),
            pltpu.VMEM((n_src, n_ids, rows, nv), bf16),
            pltpu.VMEM((HALF, n_ids, rows, nv), bf16),
            pltpu.VMEM((2, 2 * n_src, n_ids, rows, nv), bf16),
            pltpu.VMEM((2, per, n_snk, cols, nv), bf16),
            pltpu.VMEM((per, nv, nv), bf16),
            pltpu.VMEM((NSN, per, 2, 2, nv, nv // 2), f32),
            pltpu.VMEM((n_ids - NSN, per, 2, 2, 2, nv // 2, nv // 2), f32),
            pltpu.VMEM((sinks, 2 * n_diag, 128), f32),
            sem((4,)), sem((2,)), sem((2,)), sem, sem((4,)), sem((4,)),
        ]
        + [sem((2, n_src))] * 4
        + [sem((n_src,))] * 2
        + [sem((4,))] * 2,
        compiler_params=pltpu.CompilerParams(
            collective_id=0, has_side_effects=True, vmem_limit_bytes=67043328
        ),
    )(need_ids, jnp.transpose(diagrams, (2, 0, 1)), phases, block_sizes, tau_cols, elementals)
    return jnp.sum(partial, axis=2).reshape(1, 1, MAXB, 2, n_diag)


def local(tau_cols, elementals, *rest):
    fits = (
        lax.axis_size("snk") == 4
        and lax.axis_size("src") == 8
        and elementals.shape[0] == 32
        and tau_cols.shape[3] % 16 == 0
        and tau_cols.shape[4] == 256
    )
    return (fused_local if fits else plain_local)(tau_cols, elementals, *rest)


def solution(mesh):
    placed = (
        P(None, "src", None, "snk", None),
        P("src", None, None, None),
        P(),
        P("src", None, None),
        P(),
        P(),
    )
    return jax.shard_map(
        local,
        mesh=mesh,
        in_specs=placed,
        out_specs=P("src", "snk", None, None, None),
        check_vma=False,
    )
```
